32 devices in a mesh: slab: 4 (over x, core), dir: 8 (over z, y).
Axes of the slice: x: 2, y: 2, z: 4, core: 2. Of those that a mesh axis runs over, the one named last changes fastest.
Arguments:
- currents: float32 [2, 64, 128, 256], P(None, ('slab', 'dir')), may hold values from -6 to 6
- near_blocks: float32 [2, 64, 9, 128, 128], P(None, ('slab', 'dir')), may hold values from -0.1875 to 0.1875
- near_index: int32 [64, 9], P(('slab', 'dir')), may hold values from 0 to 5
- aggregate: float32 [2, 256, 128], replicated, may hold values from -0.5 to 0.5
- translations: float32 [2, 64, 256], P(None, None, 'dir'), may hold values from -1 to 1
- inter_source: int32 [64, 32], P('slab'), may hold values from 0 to 47
- inter_shift: int32 [64, 32], P('slab'), may hold values from 0 to 63
- disaggregate: float32 [2, 128, 256], replicated, may hold values from -0.375 to 0.375
Outputs:
- product: float32 [2, 64, 128, 256], P(None, ('slab', 'dir'))
The draws below stay inside these ranges and needn't reach their ends.
All inputs are finite; a program needn't handle non-finite values.
Results may differ from the reference program's by a relative error of at most 0.0003.
Values sent between devices are 32-bit elements; how exact they have to be, the bound alone decides.
A program may use at most 64 MiB of HBM per device.

```python
import jax
import jax.numpy as jnp
from jax import lax

P_SIZE = 128
K = 256
R = 256
BOX_DEV = 2
NN = 9
NI = 32
NT = 64
SLAB_BOXES = 16
BOXES = 64
N_SLAB = 4


def set_ends(drawn, stream_key, low, top_value):
    place = [jax.random.randint(jax.random.fold_in(stream_key, axis), (), 0, length) for axis, length in enumerate(drawn.shape)]
    widest = drawn.shape.index(max(drawn.shape))
    beside = place[:widest] + [(place[widest] + 1) % drawn.shape[widest]] + place[widest + 1:]
    return drawn.at[tuple(place)].set(low).at[tuple(beside)].set(top_value)


def block_scale(stream_key, extent, cuts, least, top_value):
    factor_of = 1.0
    for dim, blocks in cuts:
        steps = jax.random.uniform(jax.random.fold_in(jax.random.fold_in(stream_key, 6), dim), (blocks,), jnp.float32, least / len(cuts), top_value / len(cuts))
        factor_of = factor_of * jnp.repeat(jnp.exp(steps), extent[dim] // blocks).reshape((-1,) + (1,) * (len(extent) - 1 - dim))
    return factor_of


def centred(rng, dims, scale, reach, cuts=(), kind=jnp.bfloat16):
    entries = scale * jax.random.normal(rng, dims, jnp.float32)
    if cuts:
        entries = entries * block_scale(rng, dims, cuts, -0.22, 0.18)
    return jnp.clip(entries, -reach, reach).astype(kind)


def setup_inputs(seed: int = 0) -> dict:
    streams_of = jax.random.split(jax.random.key(seed), 9)
    return {
        "currents": centred(streams_of[0], (2, BOXES, P_SIZE, R), 1.0, 6.0, ((1, 32),), jnp.float32),
        "near_blocks": centred(streams_of[1], (2, BOXES, NN, P_SIZE, P_SIZE), (NN * P_SIZE) ** -0.5, 0.1875, ((1, 32),), jnp.float32),
        "near_index": set_ends(jax.random.randint(streams_of[2], (BOXES, NN), 0, 3 * BOX_DEV), jax.random.fold_in(streams_of[2], 1), 0, (3 * BOX_DEV) - 1).astype(jnp.int32),
        "aggregate": centred(streams_of[3], (2, K, P_SIZE), P_SIZE ** -0.5, 0.5, (), jnp.float32),
        "translations": centred(streams_of[4], (2, NT, K), 0.18, 1.0, ((2, 8),), jnp.float32),
        "inter_source": set_ends(jax.random.randint(streams_of[5], (BOXES, NI), 0, 3 * SLAB_BOXES), jax.random.fold_in(streams_of[5], 1), 0, (3 * SLAB_BOXES) - 1).astype(jnp.int32),
        "inter_shift": set_ends(jax.random.randint(streams_of[6], (BOXES, NI), 0, NT), jax.random.fold_in(streams_of[6], 1), 0, NT - 1).astype(jnp.int32),
        "disaggregate": centred(streams_of[7], (2, P_SIZE, K), K ** -0.5, 0.375, (), jnp.float32),
    }


def cein(form, left, right):
    def single(u, v):
        return jnp.einsum(form, u, v, precision=lax.Precision.HIGHEST)
    real = single(left[0], right[0]) - single(left[1], right[1])
    imag = single(left[0], right[1]) + single(left[1], right[0])
    return jnp.stack([real, imag])


def reference(currents, near_blocks, near_index, aggregate, translations, inter_source, inter_shift, disaggregate):
    def near_one(box):
        slab_id = box // SLAB_BOXES
        within = box % SLAB_BOXES
        device = within // BOX_DEV
        source = slab_id * SLAB_BOXES + (device * BOX_DEV - BOX_DEV + near_index[box] + SLAB_BOXES) % SLAB_BOXES
        pieces = jnp.take(currents, source.astype(jnp.int32), axis=1)
        blocks = jnp.take(near_blocks, box, axis=1)
        return cein('jpq,jqr->pr', blocks, pieces)

    near = lax.map(near_one, jnp.arange(BOXES, dtype=jnp.int32))
    near = jnp.transpose(near, (1, 0, 2, 3))
    radiated = cein('kp,bpr->bkr', aggregate, currents)
    zeros_rim = jnp.zeros((2, SLAB_BOXES, K, R), jnp.float32)
    padded = jnp.concatenate([zeros_rim, radiated, zeros_rim], axis=1)

    def far_slab(slab_id):
        start = (slab_id * SLAB_BOXES).astype(jnp.int32)
        local = lax.dynamic_slice_in_dim(padded, start, 3 * SLAB_BOXES, 1)
        sources = lax.dynamic_slice_in_dim(inter_source, start, SLAB_BOXES, 0)
        shifts = lax.dynamic_slice_in_dim(inter_shift, start, SLAB_BOXES, 0)

        def add_entry(entry, total):
            rows = jnp.take(local, sources[:, entry], axis=1)
            factor = jnp.take(translations, shifts[:, entry], axis=1)[:, :, :, None]
            real = factor[0] * rows[0] - factor[1] * rows[1]
            imag = factor[0] * rows[1] + factor[1] * rows[0]
            return total + jnp.stack([real, imag])

        incoming = lax.fori_loop(0, NI, add_entry, jnp.zeros((2, SLAB_BOXES, K, R), jnp.float32))
        return cein('pk,bkr->bpr', disaggregate, incoming)

    far = lax.map(far_slab, jnp.arange(N_SLAB, dtype=jnp.int32))
    far = jnp.transpose(far, (1, 0, 2, 3, 4)).reshape(2, BOXES, P_SIZE, R)
    return near + far
```

```python
import functools

import jax
import jax.numpy as jnp
from jax import lax
from jax.experimental import pallas as pl
from jax.experimental.pallas import tpu as pltpu
from jax.sharding import PartitionSpec as P

MESH = pl.DeviceIdType.MESH
CHUNKS = 1


def split(x):
    hi = x.astype(jnp.bfloat16)
    lo = (x - hi.astype(jnp.float32)).astype(jnp.bfloat16)
    return hi, lo


def dot3(left, right):
    def single(u, v):
        return jnp.dot(u, v, preferred_element_type=jnp.float32)

    return single(left[0], right[0]) + (single(left[0], right[1]) + single(left[1], right[0]))


def complex_weights(real, imag):
    return jnp.concatenate(
        [jnp.concatenate([real, imag], axis=1), jnp.concatenate([-imag, real], axis=1)], axis=0
    )


def kernel(
    slabs, dirs, chunks,
    cur_hbm, near_hbm, near_index_hbm, aggregate_hbm, trans_hbm, source_hbm, shift_hbm, disaggregate_hbm,
    out,
    cur, near_index, aggregate, trans, inter_source, inter_shift, disaggregate, input_sem,
    near_blocks, near_hi, near_lo, near_src, near_turned, w_hi, w_lo,
    own_t, cells, trans_own, trans_all, rows, tables, agg_hi, agg_lo, dis_hi, dis_lo,
    x, inc, far_out, far_in,
    fwd_send, fwd_recv, slab_send, slab_recv, tr_send, tr_recv, ts_send, ts_recv,
    nb_send, nb_recv, ng_send, ng_recv, ret_send, ret_recv,
):
    slab = lax.axis_index("slab")
    me = lax.axis_index("dir")
    box_dev, p_size, illum = cur.shape[1:]
    nn = near_hbm.shape[2]
    k_size = aggregate.shape[1]
    nt = trans.shape[2]
    slab_boxes, ni = inter_source.shape
    rc = own_t.shape[4]
    rs = rc * chunks
    has_prev = slab > 0
    has_next = slab < slabs - 1
    shares = trans_all.shape[1]
    share = slab if shares > 1 else 0
    odd = lax.rem(me, 2)
    partner = me + 1 - 2 * odd

    def across(d):
        return lax.rem(d + 2 * lax.rem(d, 2) - 1 + dirs, dirs)

    barrier = pltpu.get_barrier_semaphore()

    @pl.loop(1, dirs)
    def _(o):
        pl.semaphore_signal(barrier, inc=1, device_id={"dir": lax.rem(me + o, dirs)}, device_id_type=MESH)

    @pl.loop(1, slabs)
    def _(o):
        pl.semaphore_signal(barrier, inc=1, device_id={"slab": lax.rem(slab + o, slabs)}, device_id_type=MESH)

    cur_copy, trans_copy, *later_copies = [
        pltpu.make_async_copy(source, target, input_sem.at[i])
        for i, (source, target) in enumerate([
            (cur_hbm, cur), (trans_hbm, trans), (aggregate_hbm, aggregate),
            (disaggregate_hbm, disaggregate), (source_hbm, inter_source),
            (shift_hbm, inter_shift), (near_index_hbm, near_index), (near_hbm, near_blocks),
        ])
    ]
    cur_copy.start()
    trans_copy.start()
    for copy in later_copies:
        copy.start()
    cur_copy.wait()

    for part in range(2):
        for b in range(box_dev):
            turned = cur[part, b].T
            for d in range(dirs):
                for c in range(chunks):
                    start = d * rs + c * rc
                    own_t[c, d, part, b] = turned[start:start + rc]
    trans_copy.wait()
    trans_own[...] = jnp.concatenate([trans[0], trans[1]], axis=1).reshape(trans_own.shape)

    pl.semaphore_wait(barrier, dirs + slabs - 2)

    def fwd_copy(c, peer, slot):
        return pltpu.make_async_remote_copy(
            src_ref=own_t.at[c, peer], dst_ref=cells.at[c, 1, slot],
            send_sem=fwd_send.at[c, peer], recv_sem=fwd_recv.at[c, slot],
            device_id={"dir": peer}, device_id_type=MESH,
        )

    def tr_copy(peer, slot):
        return pltpu.make_async_remote_copy(
            src_ref=trans_own.at[share], dst_ref=trans_all.at[slot, share],
            send_sem=tr_send.at[peer], recv_sem=tr_recv.at[slot],
            device_id={"dir": peer}, device_id_type=MESH,
        )

    def ts_copy(peer, slot):
        return pltpu.make_async_remote_copy(
            src_ref=trans_all.at[:, slot], dst_ref=trans_all.at[:, slot],
            send_sem=ts_send.at[peer], recv_sem=ts_recv.at[slot],
            device_id={"slab": peer}, device_id_type=MESH,
        )

    def ng_copy(c, d, slot):
        return pltpu.make_async_remote_copy(
            src_ref=cells.at[c, 1, d], dst_ref=near_turned.at[c, slot],
            send_sem=ng_send.at[c, d], recv_sem=ng_recv.at[c, slot],
            device_id={"dir": across(d)}, device_id_type=MESH,
        )

    def slab_copy(c, side, d):
        target = slab + 1 if side == 0 else slab - 1
        return pltpu.make_async_remote_copy(
            src_ref=cells.at[c, 1, d], dst_ref=cells.at[c, 2 * side, d],
            send_sem=slab_send.at[c, side, d], recv_sem=slab_recv.at[c, side, d],
            device_id={"slab": target}, device_id_type=MESH,
        )

    def nb_copy():
        return pltpu.make_async_remote_copy(
            src_ref=cur, dst_ref=near_src, send_sem=nb_send, recv_sem=nb_recv,
            device_id={"dir": partner}, device_id_type=MESH,
        )

    def ret_copy(c, peer, slot):
        return pltpu.make_async_remote_copy(
            src_ref=far_out.at[c, peer], dst_ref=far_in.at[c, slot],
            send_sem=ret_send.at[c, peer], recv_sem=ret_recv.at[c, slot],
            device_id={"dir": peer}, device_id_type=MESH,
        )

    def forward(c, d):
        @pl.when(has_next)
        def _():
            slab_copy(c, 0, d).start()

        @pl.when(has_prev)
        def _():
            slab_copy(c, 1, d).start()

        @pl.when(across(d) != me)
        def _():
            ng_copy(c, d, me).start()

    @pl.loop(1, dirs)
    def _(o):
        tr_copy(lax.rem(me + o, dirs), me).start()

    for c in range(chunks):
        @pl.loop(1, dirs)
        def _(o):
            peer = lax.rem(me + o, dirs)
            fwd_copy(c, peer, me).start()

    nb_copy().start()

    for c in range(chunks):
        cells[c, 1, me] = own_t[c, me]
        forward(c, me)

    trans_all[me, share] = trans_own[share]

    @pl.when(jnp.logical_not(has_prev))
    def _():
        cells[:, 0] = jnp.zeros_like(cells[:, 0])

    @pl.when(jnp.logical_not(has_next))
    def _():
        cells[:, 2] = jnp.zeros_like(cells[:, 2])

    for copy in later_copies:
        copy.wait()
    agg_hi[...], agg_lo[...] = split(complex_weights(aggregate[0].T, aggregate[1].T))
    dis_hi[...], dis_lo[...] = split(complex_weights(disaggregate[0].T, disaggregate[1].T))

    @pl.loop(1, dirs)
    def _(o):
        peer = lax.rem(me + dirs - o, dirs)
        tr_copy(peer, peer).wait_recv()

    if shares > 1:
        @pl.loop(1, slabs)
        def _(o):
            ts_copy(lax.rem(slab + o, slabs), slab).start()

    for b in range(box_dev):
        @pl.loop(0, nn)
        def _(j):
            pair = jnp.concatenate([near_blocks[0, b, j], near_blocks[1, b, j]], axis=1)
            near_hi[b, j], near_lo[b, j] = split(pair)

    def radiate(c, g):
        count = dirs * box_dev * rc
        pair = jnp.concatenate(
            [cells[c, g, :, part].reshape(count, p_size) for part in range(2)], axis=1
        )
        y = dot3(split(pair), (agg_hi[...], agg_lo[...]))
        re = y[:, :k_size].reshape(slab_boxes, rc // 8, 8, k_size)
        im = y[:, k_size:].reshape(slab_boxes, rc // 8, 8, k_size)
        boxes = pl.ds(g * slab_boxes, slab_boxes)
        x[0, boxes] = re
        x[1, boxes] = im
        x[2, boxes] = re + im

    def far_device(c, owner):
        for bb in range(box_dev):
            b = owner * box_dev + bb

            def entry(i, sums):
                s1, s2, s3 = sums
                src = inter_source[b, i]
                shift = inter_shift[b, i]
                s1 = s1 + tables[0, shift] * x[2, src]
                s2 = s2 + tables[1, shift] * x[1, src]
                s3 = s3 + tables[2, shift] * x[0, src]
                return s1, s2, s3

            zero = jnp.zeros((rc // 8, 8, k_size), jnp.float32)
            s1, s2, s3 = lax.fori_loop(0, ni, entry, (zero, zero, zero), unroll=4)
            here = slice(bb * rc, (bb + 1) * rc)
            inc[here, :k_size] = (s1 - s2).reshape(rc, k_size)
            inc[here, k_size:] = (s1 + s3).reshape(rc, k_size)
        y = dot3(split(inc[...]), (dis_hi[...], dis_lo[...]))
        far_out[c, owner, 0] = y[:, :p_size].reshape(box_dev, rc, p_size)
        far_out[c, owner, 1] = y[:, p_size:].reshape(box_dev, rc, p_size)

    for c in range(chunks):
        @pl.loop(1, dirs)
        def _(o):
            peer = lax.rem(me + dirs - o, dirs)
            fwd_copy(c, peer, peer).wait_recv()
            forward(c, peer)

        if c == 0:
            if shares > 1:
                @pl.loop(1, slabs)
                def _(o):
                    peer = lax.rem(slab + slabs - o, slabs)
                    ts_copy(peer, peer).wait_recv()

            turned = trans_all[...].reshape(k_size, 2 * nt).T
            rows[0] = turned[:nt]
            rows[1] = turned[:nt] + turned[nt:]
            rows[2] = turned[nt:] - turned[:nt]

            @pl.loop(0, nt)
            def _(t):
                for f in range(3):
                    tables[f, t] = jnp.broadcast_to(rows[f, pl.ds(t, 1), :], (8, k_size))

        radiate(c, 1)

        @pl.when(has_prev)
        def _():
            @pl.loop(0, dirs)
            def _(d):
                slab_copy(c, 0, d).wait_recv()

        radiate(c, 0)

        @pl.when(has_next)
        def _():
            @pl.loop(0, dirs)
            def _(d):
                slab_copy(c, 1, d).wait_recv()

        radiate(c, 2)

        @pl.loop(1, dirs + 1)
        def _(o):
            owner = lax.rem(me + o, dirs)
            far_device(c, owner)

            @pl.when(o < dirs)
            def _():
                ret_copy(c, owner, me).start()

        far_in[c, me] = far_out[c, me]

    def near_weights(group, b, real, imag):
        w_hi[group * box_dev + b], w_lo[group * box_dev + b] = split(complex_weights(real, imag))

    def whole(ref, part, b):
        pieces = [ref[c, d, part, b] for d in range(dirs) for c in range(chunks)]
        return jnp.concatenate(pieces, axis=0).T

    nb_copy().wait_recv()
    for b in range(box_dev):
        near_weights(1, b, cur[0, b], cur[1, b])
        near_weights(2 - 2 * odd, b, near_src[0, b], near_src[1, b])

    for c in range(chunks):
        near_turned[c, me] = cells[c, 1, across(me)]

        @pl.loop(1, dirs)
        def _(o):
            slot = lax.rem(me + dirs - o, dirs)
            ng_copy(c, across(me), slot).wait_recv()

    for b in range(box_dev):
        near_weights(2 * odd, b, whole(near_turned, 0, b), whole(near_turned, 1, b))

    @pl.loop(0, box_dev)
    def _(b):
        total = jnp.zeros((p_size, 2 * illum), jnp.float32)
        for j in range(nn):
            src = near_index[b, j]
            total = total + dot3((near_hi[b, j], near_lo[b, j]), (w_hi[src], w_lo[src]))
        out[0, b] = total[:, :illum]
        out[1, b] = total[:, illum:]

    for c in range(chunks):
        @pl.loop(1, dirs)
        def _(o):
            peer = lax.rem(me + dirs - o, dirs)
            ret_copy(c, peer, peer).wait_recv()

    for part in range(2):
        for b in range(box_dev):
            out[part, b] += whole(far_in, part, b)

    for c in range(chunks):
        @pl.loop(1, dirs)
        def _(o):
            peer = lax.rem(me + o, dirs)
            fwd_copy(c, peer, me).wait_send()
            ret_copy(c, peer, me).wait_send()
            if c == 0:
                tr_copy(peer, me).wait_send()

        @pl.loop(0, dirs)
        def _(d):
            @pl.when(across(d) != me)
            def _():
                ng_copy(c, d, me).wait_send()

        @pl.when(has_next)
        def _():
            @pl.loop(0, dirs)
            def _(d):
                slab_copy(c, 0, d).wait_send()

        @pl.when(has_prev)
        def _():
            @pl.loop(0, dirs)
            def _(d):
                slab_copy(c, 1, d).wait_send()

    if shares > 1:
        @pl.loop(1, slabs)
        def _(o):
            ts_copy(lax.rem(slab + o, slabs), slab).wait_send()

    nb_copy().wait_send()


def body(slabs, dirs, *args):
    cur, near_blocks, near_index, aggregate, trans, inter_source, inter_shift, disaggregate = args
    box_dev, p_size, illum = cur.shape[1:]
    nn = near_blocks.shape[2]
    k_size = aggregate.shape[1]
    nt, k_loc = trans.shape[1:]
    slab_boxes = inter_source.shape[0]
    rs = illum // dirs
    chunks = CHUNKS if rs % (8 * CHUNKS) == 0 else 1
    rc = rs // chunks
    shares = slabs if k_loc % (8 * slabs) == 0 else 1
    f32, bf16 = jnp.float32, jnp.bfloat16
    vmem = pl.BlockSpec(memory_space=pltpu.VMEM)
    sem = pltpu.SemaphoreType.DMA
    return pl.pallas_call(
        functools.partial(kernel, slabs, dirs, chunks),
        out_shape=jax.ShapeDtypeStruct(cur.shape, f32),
        in_specs=[pl.BlockSpec(memory_space=pltpu.HBM)] * 8,
        out_specs=vmem,
        scratch_shapes=[
            pltpu.VMEM(cur.shape, f32),
            pltpu.SMEM(near_index.shape, jnp.int32),
            pltpu.VMEM(aggregate.shape, f32),
            pltpu.VMEM((2, k_loc, nt), f32),
            pltpu.SMEM(inter_source.shape, jnp.int32),
            pltpu.SMEM(inter_shift.shape, jnp.int32),
            pltpu.VMEM(disaggregate.shape, f32),
            sem((8,)),
            pltpu.VMEM(near_blocks.shape, f32),
            pltpu.VMEM((box_dev, nn, p_size, 2 * p_size), bf16),
            pltpu.VMEM((box_dev, nn, p_size, 2 * p_size), bf16),
            pltpu.VMEM(cur.shape, f32),
            pltpu.VMEM((chunks, dirs, 2, box_dev, rc, p_size), f32),
            pltpu.VMEM((3 * box_dev, 2 * p_size, 2 * illum), bf16),
            pltpu.VMEM((3 * box_dev, 2 * p_size, 2 * illum), bf16),
            pltpu.VMEM((chunks, dirs, 2, box_dev, rc, p_size), f32),
            pltpu.VMEM((chunks, 3, dirs, 2, box_dev, rc, p_size), f32),
            pltpu.VMEM((shares, k_loc // shares, 2 * nt), f32),
            pltpu.VMEM((dirs, shares, k_loc // shares, 2 * nt), f32),
            pltpu.VMEM((3, nt, k_size), f32),
            pltpu.VMEM((3, nt, 8, k_size), f32),
            pltpu.VMEM((2 * p_size, 2 * k_size), bf16),
            pltpu.VMEM((2 * p_size, 2 * k_size), bf16),
            pltpu.VMEM((2 * k_size, 2 * p_size), bf16),
            pltpu.VMEM((2 * k_size, 2 * p_size), bf16),
            pltpu.VMEM((3, 3 * slab_boxes, rc // 8, 8, k_size), f32),
            pltpu.VMEM((box_dev * rc, 2 * k_size), f32),
            pltpu.VMEM((chunks, dirs, 2, box_dev, rc, p_size), f32),
            pltpu.VMEM((chunks, dirs, 2, box_dev, rc, p_size), f32),
            sem((chunks, dirs)), sem((chunks, dirs)),
            sem((chunks, 2, dirs)), sem((chunks, 2, dirs)),
            sem((dirs,)), sem((dirs,)),
            sem((slabs,)), sem((slabs,)),
            sem(()), sem(()),
            sem((chunks, dirs)), sem((chunks, dirs)),
            sem((chunks, dirs)), sem((chunks, dirs)),
        ],
        compiler_params=pltpu.CompilerParams(
            collective_id=0, has_side_effects=True, vmem_limit_bytes=48 * 2**20
        ),
    )(*[pltpu.with_memory_space_constraint(v, pltpu.HBM) for v in (
        cur, near_blocks, near_index, aggregate, jnp.swapaxes(trans, 1, 2), inter_source, inter_shift, disaggregate)])


def solution(mesh):
    in_specs = (
        P(None, ("slab", "dir"), None, None),
        P(None, ("slab", "dir"), None, None, None),
        P(("slab", "dir"), None),
        P(),
        P(None, None, "dir"),
        P("slab", None),
        P("slab", None),
        P(),
    )
    out_specs = P(None, ("slab", "dir"), None, None)
    run = functools.partial(body, mesh.shape["slab"], mesh.shape["dir"])
    return jax.shard_map(run, mesh=mesh, in_specs=in_specs, out_specs=out_specs, check_vma=False)
```

```python
import functools

import jax
import jax.numpy as jnp
from jax import lax
from jax.experimental import pallas as pl
from jax.experimental.pallas import tpu as pltpu
from jax.sharding import PartitionSpec as P

MESH = pl.DeviceIdType.MESH


def split(x):
    hi = x.astype(jnp.bfloat16)
    lo = (x - hi.astype(jnp.float32)).astype(jnp.bfloat16)
    return hi, lo


def dot3(left, right):
    def single(u, v):
        return jnp.dot(u, v, preferred_element_type=jnp.float32)

    return single(left[0], right[0]) + (single(left[0], right[1]) + single(left[1], right[0]))


def complex_weights(real, imag):
    return jnp.concatenate(
        [jnp.concatenate([real, imag], axis=1), jnp.concatenate([-imag, real], axis=1)], axis=0
    )


def plan(illum, zs):
    half = illum // 2
    return ((zs, half // zs, 0),)


def kernel(
    slabs, dirs, chunks,
    cur_hbm, near_hbm, near_index_hbm, aggregate_hbm, trans_hbm, source_hbm, shift_hbm, disaggregate_hbm,
    out,
    cur, near_index, aggregate, trans, inter_source, inter_shift, disaggregate, input_sem,
    near_blocks, near_hi, near_lo, near_par, near_turned, w_hi, w_lo,
    own_t, par_t, far_all, trans_own, trans_all, rows, tables, agg_hi, agg_lo, dis_hi, dis_lo,
    cells, x, inc, far_out,
    hand, first_send, first_recv, line_send, relay_send, line_recv, slab_send, slab_recv,
    tr_send, tr_recv, ts_send, ts_recv, nb_send, nb_recv, ng_send, ng_recv,
    na_send, na_recv, nr_send, nr_recv, ret_send, ret_recv,
):
    slab = lax.axis_index("slab")
    me = lax.axis_index("dir")
    box_dev, p_size, illum = cur.shape[1:]
    nn = near_hbm.shape[2]
    k_size = aggregate.shape[1]
    nt = trans.shape[2]
    slab_boxes, ni = inter_source.shape
    has_prev = slab > 0
    has_next = slab < slabs - 1
    shares = trans_all.shape[1]
    share = slab if shares > 1 else 0
    zs = dirs // 2
    zh = zs // 2
    hr = illum // 2
    z = me // 2
    y = lax.rem(me, 2)
    partner = 2 * z + 1 - y
    has_lower = z > 0
    has_upper = z < zs - 1
    inward = 1 - 2 * (z // zh)

    def toward(o):
        return lax.rem(z + inward * o + zs, zs)

    def across(d):
        return lax.rem(d + 2 * lax.rem(d, 2) - 1 + dirs, dirs)

    def row(c, side, i):
        nz, rc, off = chunks[c]
        return pl.multiple_of(side * hr + off + lax.rem(i, nz) * rc, 8)

    def my_rows(c, side, i):
        return pl.ds(row(c, side, i), chunks[c][1])

    barrier = pltpu.get_barrier_semaphore()

    def greet(sem, peer):
        pl.semaphore_signal(sem, inc=1, device_id={"dir": peer}, device_id_type=MESH)

    greet(barrier, partner)

    @pl.when(has_lower)
    def _():
        greet(barrier, me - 2)

    @pl.when(has_upper)
    def _():
        greet(barrier, me + 2)

    @pl.loop(1, slabs)
    def _(o):
        pl.semaphore_signal(barrier, inc=1, device_id={"slab": lax.rem(slab + o, slabs)}, device_id_type=MESH)

    cur_copy, trans_copy, *later_copies = [
        pltpu.make_async_copy(source, target, input_sem.at[i])
        for i, (source, target) in enumerate([
            (cur_hbm, cur), (trans_hbm, trans), (aggregate_hbm, aggregate),
            (disaggregate_hbm, disaggregate), (source_hbm, inter_source),
            (shift_hbm, inter_shift), (near_index_hbm, near_index), (near_hbm, near_blocks),
        ])
    ]
    cur_copy.start()
    trans_copy.start()
    for copy in later_copies:
        copy.start()
    cur_copy.wait()

    for part in range(2):
        for b in range(box_dev):
            own_t[part, b] = cur[part, b].T
    trans_copy.wait()
    trans_own[...] = jnp.concatenate([trans[0], trans[1]], axis=1).reshape(trans_own.shape)

    def remote(src, dst, send, recv, **peer):
        return pltpu.make_async_remote_copy(
            src_ref=src, dst_ref=dst, send_sem=send, recv_sem=recv, device_id=peer, device_id_type=MESH
        )

    def first_copy(c, i, side):
        return remote(
            own_t.at[:, :, my_rows(c, side, i)], par_t.at[:, :, my_rows(c, 0, i)],
            first_send.at[c, i], first_recv.at[c, i], dir=partner,
        )

    def line_copy(c, peer, slot):
        return remote(
            own_t.at[:, :, my_rows(c, y, peer // 2)], cells[c].at[1, slot],
            line_send.at[c, peer // 2], line_recv.at[c, slot], dir=peer,
        )

    def relay_copy(c, peer, slot):
        return remote(
            par_t.at[:, :, my_rows(c, 0, peer // 2)], cells[c].at[1, slot],
            relay_send.at[c, peer // 2], line_recv.at[c, slot], dir=peer,
        )

    def tr_copy(peer, slot):
        return remote(
            trans_own.at[share], trans_all.at[slot, share], tr_send.at[peer], tr_recv.at[slot], dir=peer
        )

    def ts_copy(peer, slot):
        return remote(
            trans_all.at[:, slot], trans_all.at[:, slot], ts_send.at[peer], ts_recv.at[slot], slab=peer
        )

    def slab_copy(c, side, d):
        target = slab + 1 if side == 0 else slab - 1
        return remote(
            cells[c].at[1, d], cells[c].at[2 * side, d],
            slab_send.at[c, side, d], slab_recv.at[c, side, d], slab=target,
        )

    def nb_copy(side):
        lanes = pl.ds(pl.multiple_of(side * hr, 128), hr)
        return remote(
            cur.at[:, :, :, lanes], near_par.at[:, :, :, lanes], nb_send, nb_recv, dir=partner
        )

    def ng_copy(c, d, holder):
        return remote(
            cells[c].at[1, d], near_turned.at[:, :, my_rows(c, lax.rem(holder, 2), holder // 2)],
            ng_send.at[c, d], ng_recv.at[c, holder], dir=across(d),
        )

    def apart(c, side, target):
        nz, rc, off = chunks[c]
        start = off + (1 - target // 2 // zh) * zh * rc
        return pl.ds(pl.multiple_of(side * hr + start, 8), zh * rc)

    def na_copy(c, side, target, peer):
        window = apart(c, side, target)
        return remote(
            own_t.at[:, :, window], near_turned.at[:, :, window], na_send.at[c], na_recv.at[c], dir=peer
        )

    def nr_copy(c, side, target, peer):
        return remote(
            par_t.at[:, :, apart(c, 0, target)], near_turned.at[:, :, apart(c, side, target)],
            nr_send.at[c], nr_recv.at[c], dir=peer,
        )

    def ret_copy(c, peer, sender):
        return remote(
            far_out[c].at[peer], far_all.at[:, :, my_rows(c, lax.rem(sender, 2), sender // 2)],
            ret_send.at[c, peer], ret_recv.at[c, sender], dir=peer,
        )

    def same_half(d):
        return d // 2 // zh == z // zh

    def passes_on(d):
        return jnp.logical_and(same_half(across(d)), across(d) != me)

    def forward(c, d):
        @pl.when(has_next)
        def _():
            slab_copy(c, 0, d).start()

        @pl.when(has_prev)
        def _():
            slab_copy(c, 1, d).start()

    def stage(s):
        @pl.when(has_upper)
        def _():
            greet(hand.at[s, 0], me + 2)

        @pl.when(has_lower)
        def _():
            greet(hand.at[s, 1], me - 2)

    def staged(s):
        @pl.when(has_lower)
        def _():
            pl.semaphore_wait(hand.at[s, 0], 1)

        @pl.when(has_upper)
        def _():
            pl.semaphore_wait(hand.at[s, 1], 1)

    def along(o):
        @pl.when(z + o < zs)
        def _():
            tr_copy(me + 2 * o, me).start()
            for c in range(len(chunks)):
                line_copy(c, me + 2 * o, me).start()

        @pl.when(z - o >= 0)
        def _():
            tr_copy(me - 2 * o, me).start()
            for c in range(len(chunks)):
                line_copy(c, me - 2 * o, me).start()

    def askew(o):
        @pl.when(z + o < zs)
        def _():
            tr_copy(partner + 2 * o, me).start()

        @pl.when(z - o >= 0)
        def _():
            tr_copy(partner - 2 * o, me).start()

    pl.semaphore_wait(barrier, slabs + (z + zs - 1) // zs + (2 * zs - 2 - z) // zs)
    stage(0)
    for c, (nz, rc, off) in enumerate(chunks):
        for o in range(nz):
            first_copy(c, lax.rem(toward(o + 1), nz), 1 - y).start()
    tr_copy(partner, me).start()
    along(1)
    nb_copy(y).start()
    for c in range(len(chunks)):
        cells[c][1, me] = own_t[:, :, my_rows(c, y, z)]
        forward(c, me)
    for o in range(2, zs):
        staged(o - 2)
        stage(o - 1)
        askew(o - 1)
        along(o)
    staged(zs - 2)
    askew(zs - 1)

    for copy in later_copies:
        copy.wait()
    agg_hi[...], agg_lo[...] = split(complex_weights(aggregate[0].T, aggregate[1].T))
    dis_hi[...], dis_lo[...] = split(complex_weights(disaggregate[0].T, disaggregate[1].T))

    for c, (nz, rc, off) in enumerate(chunks):
        for o in range(nz):
            i = lax.rem(toward(o + 1), nz)
            first_copy(c, i, 1 - y).wait_recv()
            for g in range(zs // nz):
                @pl.when(i + g * nz != z)
                def _():
                    relay_copy(c, 2 * (i + g * nz) + y, partner).start()

        cells[c][1, partner] = par_t[:, :, my_rows(c, 0, z)]
        forward(c, partner)

    trans_all[me, share] = trans_own[share]

    @pl.when(jnp.logical_not(has_prev))
    def _():
        for c in range(len(chunks)):
            cells[c][0] = jnp.zeros_like(cells[c][0])

    @pl.when(jnp.logical_not(has_next))
    def _():
        for c in range(len(chunks)):
            cells[c][2] = jnp.zeros_like(cells[c][2])

    @pl.loop(1, dirs)
    def _(o):
        peer = lax.rem(me + dirs - o, dirs)
        tr_copy(peer, peer).wait_recv()

    if shares > 1:
        @pl.loop(1, slabs)
        def _(o):
            ts_copy(lax.rem(slab + o, slabs), slab).start()

    steps = 2 * (zs - 1) * len(chunks)
    load = -(-box_dev * nn // steps)

    def split_near(t):
        @pl.loop(t * load, jnp.minimum((t + 1) * load, box_dev * nn))
        def _(q):
            b, j = q // nn, lax.rem(q, nn)
            pair = jnp.concatenate([near_blocks[0, b, j], near_blocks[1, b, j]], axis=1)
            near_hi[b, j], near_lo[b, j] = split(pair)

    def radiate(c, g):
        rc = chunks[c][1]
        count = dirs * box_dev * rc
        pair = jnp.concatenate(
            [cells[c][g, :, part].reshape(count, p_size) for part in range(2)], axis=1
        )
        w = dot3(split(pair), (agg_hi[...], agg_lo[...]))
        re = w[:, :k_size].reshape(slab_boxes, rc // 8, 8, k_size)
        im = w[:, k_size:].reshape(slab_boxes, rc // 8, 8, k_size)
        boxes = pl.ds(g * slab_boxes, slab_boxes)
        x[c][0, boxes] = re
        x[c][1, boxes] = im
        x[c][2, boxes] = re + im

    def far_device(c, owner):
        rc = chunks[c][1]
        step = min(rc // 8, 4)
        for bb in range(box_dev):
            b = owner * box_dev + bb
            for r in range(0, rc // 8, step):
                block = pl.ds(r, step)

                def entry(i, sums):
                    s1, s2, s3 = sums
                    src = inter_source[b, i]
                    shift = inter_shift[b, i]
                    s1 = s1 + tables[0, shift] * x[c][2, src, block]
                    s2 = s2 + tables[1, shift] * x[c][1, src, block]
                    s3 = s3 + tables[2, shift] * x[c][0, src, block]
                    return s1, s2, s3

                zero = jnp.zeros((step, 8, k_size), jnp.float32)
                s1, s2, s3 = lax.fori_loop(0, ni, entry, (zero, zero, zero), unroll=4)
                here = slice(bb * rc + 8 * r, bb * rc + 8 * (r + step))
                inc[c][here, :k_size] = (s1 - s2).reshape(8 * step, k_size)
                inc[c][here, k_size:] = (s1 + s3).reshape(8 * step, k_size)
        w = dot3(split(inc[c][...]), (dis_hi[...], dis_lo[...]))
        far_out[c][owner, 0] = w[:, :p_size].reshape(box_dev, rc, p_size)
        far_out[c][owner, 1] = w[:, p_size:].reshape(box_dev, rc, p_size)

    for c, (nz, rc, off) in enumerate(chunks):
        for turn, side in enumerate((y, 1 - y)):
            @pl.loop(1, zs)
            def _(o):
                peer = 2 * lax.rem(z + o, zs) + side
                line_copy(c, peer, peer).wait_recv()
                forward(c, peer)
                split_near((2 * c + turn) * (zs - 1) + o - 1)

        if nz == zs:
            na_copy(c, y, across(me), across(me)).start()
            nr_copy(c, y, across(partner), across(partner)).start()

        @pl.loop(0, dirs)
        def _(d):
            @pl.when(passes_on(d))
            def _():
                ng_copy(c, d, me).start()

        if c == 0:
            if shares > 1:
                @pl.loop(1, slabs)
                def _(o):
                    peer = lax.rem(slab + slabs - o, slabs)
                    ts_copy(peer, peer).wait_recv()

            turned = trans_all[...].reshape(k_size, 2 * nt).T
            rows[0] = turned[:nt]
            rows[1] = turned[:nt] + turned[nt:]
            rows[2] = turned[nt:] - turned[:nt]

            @pl.loop(0, nt)
            def _(t):
                for f in range(3):
                    tables[f, t] = jnp.broadcast_to(rows[f, pl.ds(t, 1), :], (8, k_size))

        radiate(c, 1)

        @pl.when(has_prev)
        def _():
            @pl.loop(0, dirs)
            def _(d):
                slab_copy(c, 0, d).wait_recv()

        radiate(c, 0)

        @pl.when(has_next)
        def _():
            @pl.loop(0, dirs)
            def _(d):
                slab_copy(c, 1, d).wait_recv()

        radiate(c, 2)
        group = 2 * nz
        base = me // group * group

        @pl.loop(0, group)
        def _(o):
            owner = base + 2 * lax.rem(toward(1 + o // 2), nz) + lax.rem(y + 1 + o, 2)
            far_device(c, owner)

            @pl.when(owner != me)
            def _():
                ret_copy(c, owner, me).start()

        far_all[:, :, my_rows(c, y, z)] = far_out[c][me]

    def near_weights(group, b, real, imag):
        w_hi[group * box_dev + b], w_lo[group * box_dev + b] = split(complex_weights(real, imag))

    for side in range(2):
        @pl.when(y == side)
        def _():
            for part in range(2):
                for b in range(box_dev):
                    near_par[part, b, :, side * hr:(side + 1) * hr] = par_t[part, b].T

    nb_copy(1 - y).wait_recv()
    for b in range(box_dev):
        near_weights(1, b, cur[0, b], cur[1, b])
        near_weights(2 - 2 * y, b, near_par[0, b], near_par[1, b])

    for c, (nz, rc, off) in enumerate(chunks):
        near_turned[:, :, my_rows(c, y, z)] = cells[c][1, across(me)]

        @pl.loop(0, 2 * zh)
        def _(o):
            holder = z // zh * zh * 2 + o

            @pl.when(holder != me)
            def _():
                ng_copy(c, across(me), holder).wait_recv()

        if nz == zs:
            na_copy(c, 1 - y, me, across(me)).wait_recv()
            nr_copy(c, y, me, across(me)).wait_recv()

    for b in range(box_dev):
        near_weights(2 * y, b, near_turned[0, b].T, near_turned[1, b].T)

    @pl.loop(0, box_dev)
    def _(b):
        total = jnp.zeros((p_size, 2 * illum), jnp.float32)
        for j in range(nn):
            src = near_index[b, j]
            total = total + dot3((near_hi[b, j], near_lo[b, j]), (w_hi[src], w_lo[src]))
        out[0, b] = total[:, :illum]
        out[1, b] = total[:, illum:]

    for c, (nz, rc, off) in enumerate(chunks):
        group = 2 * nz
        base = me // group * group

        @pl.loop(1, group)
        def _(o):
            peer = base + lax.rem(me + group - o, group)
            ret_copy(c, peer, peer).wait_recv()

    for part in range(2):
        for b in range(box_dev):
            out[part, b] += far_all[part, b].T

    for c, (nz, rc, off) in enumerate(chunks):
        group = 2 * nz
        base = me // group * group

        @pl.loop(1, group)
        def _(o):
            ret_copy(c, base + lax.rem(me + o, group), me).wait_send()

        @pl.loop(0, nz)
        def _(i):
            first_copy(c, i, 1 - y).wait_send()

        @pl.loop(1, zs)
        def _(o):
            peer = 2 * lax.rem(z + o, zs) + y
            line_copy(c, peer, me).wait_send()
            relay_copy(c, peer, partner).wait_send()

        @pl.loop(0, dirs)
        def _(d):
            @pl.when(passes_on(d))
            def _():
                ng_copy(c, d, me).wait_send()

        if nz == zs:
            na_copy(c, y, across(me), across(me)).wait_send()
            nr_copy(c, y, across(partner), across(partner)).wait_send()

        @pl.when(has_next)
        def _():
            @pl.loop(0, dirs)
            def _(d):
                slab_copy(c, 0, d).wait_send()

        @pl.when(has_prev)
        def _():
            @pl.loop(0, dirs)
            def _(d):
                slab_copy(c, 1, d).wait_send()

    @pl.loop(1, dirs)
    def _(o):
        tr_copy(lax.rem(me + o, dirs), me).wait_send()

    if shares > 1:
        @pl.loop(1, slabs)
        def _(o):
            ts_copy(lax.rem(slab + o, slabs), slab).wait_send()

    nb_copy(y).wait_send()


def body(slabs, dirs, *args):
    cur, near_blocks, near_index, aggregate, trans, inter_source, inter_shift, disaggregate = args
    box_dev, p_size, illum = cur.shape[1:]
    nn = near_blocks.shape[2]
    k_size = aggregate.shape[1]
    nt, k_loc = trans.shape[1:]
    slab_boxes = inter_source.shape[0]
    zs = dirs // 2
    chunks = plan(illum, zs)
    n = len(chunks)
    shares = slabs if k_loc % (8 * slabs) == 0 else 1
    f32, bf16 = jnp.float32, jnp.bfloat16
    vmem = pl.BlockSpec(memory_space=pltpu.VMEM)
    sem = pltpu.SemaphoreType.DMA
    turned = pltpu.VMEM((2, box_dev, illum, p_size), f32)
    operands = (
        cur, near_blocks, near_index, aggregate, jnp.swapaxes(trans, 1, 2), inter_source, inter_shift, disaggregate
    )
    return pl.pallas_call(
        functools.partial(kernel, slabs, dirs, chunks),
        out_shape=jax.ShapeDtypeStruct(cur.shape, f32),
        in_specs=[pl.BlockSpec(memory_space=pltpu.HBM)] * 8,
        out_specs=vmem,
        scratch_shapes=[
            pltpu.VMEM(cur.shape, f32),
            pltpu.SMEM(near_index.shape, jnp.int32),
            pltpu.VMEM(aggregate.shape, f32),
            pltpu.VMEM((2, k_loc, nt), f32),
            pltpu.SMEM(inter_source.shape, jnp.int32),
            pltpu.SMEM(inter_shift.shape, jnp.int32),
            pltpu.VMEM(disaggregate.shape, f32),
            sem((8,)),
            pltpu.VMEM(near_blocks.shape, f32),
            pltpu.VMEM((box_dev, nn, p_size, 2 * p_size), bf16),
            pltpu.VMEM((box_dev, nn, p_size, 2 * p_size), bf16),
            pltpu.VMEM(cur.shape, f32),
            turned,
            pltpu.VMEM((3 * box_dev, 2 * p_size, 2 * illum), bf16),
            pltpu.VMEM((3 * box_dev, 2 * p_size, 2 * illum), bf16),
            turned,
            pltpu.VMEM((2, box_dev, illum // 2, p_size), f32),
            turned,
            pltpu.VMEM((shares, k_loc // shares, 2 * nt), f32),
            pltpu.VMEM((dirs, shares, k_loc // shares, 2 * nt), f32),
            pltpu.VMEM((3, nt, k_size), f32),
            pltpu.VMEM((3, nt, 8, k_size), f32),
            pltpu.VMEM((2 * p_size, 2 * k_size), bf16),
            pltpu.VMEM((2 * p_size, 2 * k_size), bf16),
            pltpu.VMEM((2 * k_size, 2 * p_size), bf16),
            pltpu.VMEM((2 * k_size, 2 * p_size), bf16),
            [pltpu.VMEM((3, dirs, 2, box_dev, rc, p_size), f32) for _, rc, _ in chunks],
            [pltpu.VMEM((3, 3 * slab_boxes, rc // 8, 8, k_size), f32) for _, rc, _ in chunks],
            [pltpu.VMEM((box_dev * rc, 2 * k_size), f32) for _, rc, _ in chunks],
            [pltpu.VMEM((dirs, 2, box_dev, rc, p_size), f32) for _, rc, _ in chunks],
            pltpu.SemaphoreType.REGULAR((zs, 2)),
            sem((n, zs)), sem((n, zs)),
            sem((n, zs)), sem((n, zs)), sem((n, dirs)),
            sem((n, 2, dirs)), sem((n, 2, dirs)),
            sem((dirs,)), sem((dirs,)),
            sem((slabs,)), sem((slabs,)),
            sem(()), sem(()),
            sem((n, dirs)), sem((n, dirs)),
            sem((n,)), sem((n,)),
            sem((n,)), sem((n,)),
            sem((n, dirs)), sem((n, dirs)),
        ],
        compiler_params=pltpu.CompilerParams(
            collective_id=0, has_side_effects=True, vmem_limit_bytes=48 * 2**20
        ),
    )(*[pltpu.with_memory_space_constraint(v, pltpu.HBM) for v in operands])


def solution(mesh):
    in_specs = (
        P(None, ("slab", "dir"), None, None),
        P(None, ("slab", "dir"), None, None, None),
        P(("slab", "dir"), None),
        P(),
        P(None, None, "dir"),
        P("slab", None),
        P("slab", None),
        P(),
    )
    out_specs = P(None, ("slab", "dir"), None, None)
    run = functools.partial(body, mesh.shape["slab"], mesh.shape["dir"])
    return jax.shard_map(run, mesh=mesh, in_specs=in_specs, out_specs=out_specs, check_vma=False)
```

```python
import functools

import jax
import jax.numpy as jnp
from jax import lax
from jax.experimental import pallas as pl
from jax.experimental.pallas import tpu as pltpu
from jax.sharding import PartitionSpec as P

MESH = pl.DeviceIdType.MESH


def split(x):
    hi = x.astype(jnp.bfloat16)
    lo = (x - hi.astype(jnp.float32)).astype(jnp.bfloat16)
    return hi, lo


def dot3(left, right):
    def single(u, v):
        return jnp.dot(u, v, preferred_element_type=jnp.float32)

    return single(left[0], right[0]) + (single(left[0], right[1]) + single(left[1], right[0]))


def complex_weights(real, imag):
    return jnp.concatenate(
        [jnp.concatenate([real, imag], axis=1), jnp.concatenate([-imag, real], axis=1)], axis=0
    )


def plan(illum, zs):
    half = illum // 2
    return ((zs, half // zs, 0),)


def kernel(
    slabs, dirs, chunks,
    cur_hbm, near_hbm, near_index_hbm, aggregate_hbm, trans_hbm, source_hbm, shift_hbm, disaggregate_hbm,
    out,
    cur, near_index, aggregate, trans, inter_source, inter_shift, disaggregate, input_sem,
    near_blocks, near_hi, near_lo, near_par, near_turned, w_hi, w_lo,
    own_t, par_t, far_all, trans_own, trans_all, rows, tables, agg_hi, agg_lo, dis_hi, dis_lo,
    cells, x, inc, far_out,
    hand, first_send, first_recv, line_send, relay_send, line_recv, slab_send, slab_recv,
    tr_send, tr_recv, ts_send, ts_recv, nb_send, nb_recv, ng_send, ng_recv,
    na_send, na_recv, nr_send, nr_recv, ret_send, ret_recv,
):
    slab = lax.axis_index("slab")
    me = lax.axis_index("dir")
    box_dev, p_size, illum = cur.shape[1:]
    nn = near_hbm.shape[2]
    k_size = aggregate.shape[1]
    nt = trans.shape[2]
    slab_boxes, ni = inter_source.shape
    has_prev = slab > 0
    has_next = slab < slabs - 1
    shares = trans_all.shape[1]
    share = slab if shares > 1 else 0
    zs = dirs // 2
    zh = zs // 2
    hr = illum // 2
    rc0 = illum // dirs
    z = me // 2
    y = lax.rem(me, 2)
    partner = 2 * z + 1 - y
    has_lower = z > 0
    has_upper = z < zs - 1
    inward = 1 - 2 * (z // zh)

    def toward(o):
        return lax.rem(z + inward * o + zs, zs)

    def across(d):
        return lax.rem(d + 2 * lax.rem(d, 2) - 1 + dirs, dirs)

    barrier = pltpu.get_barrier_semaphore()

    def greet(sem, peer):
        pl.semaphore_signal(sem, inc=1, device_id={"dir": peer}, device_id_type=MESH)

    greet(barrier, partner)

    @pl.when(has_lower)
    def _():
        greet(barrier, me - 2)

    @pl.when(has_upper)
    def _():
        greet(barrier, me + 2)

    @pl.loop(1, slabs)
    def _(o):
        pl.semaphore_signal(barrier, inc=1, device_id={"slab": lax.rem(slab + o, slabs)}, device_id_type=MESH)

    cur_copy, trans_copy, *later_copies = [
        pltpu.make_async_copy(source, target, input_sem.at[i])
        for i, (source, target) in enumerate([
            (cur_hbm, cur), (trans_hbm, trans), (aggregate_hbm, aggregate),
            (disaggregate_hbm, disaggregate), (source_hbm, inter_source),
            (shift_hbm, inter_shift), (near_index_hbm, near_index), (near_hbm, near_blocks),
        ])
    ]
    cur_copy.start()
    trans_copy.start()
    for copy in later_copies:
        copy.start()
    cur_copy.wait()

    for part in range(2):
        for b in range(box_dev):
            turned = cur[part, b].T
            for d in range(dirs):
                own_t[d // zs, d % zs, part, b] = turned[d * rc0:(d + 1) * rc0]
    trans_copy.wait()
    trans_own[...] = jnp.concatenate([trans[0], trans[1]], axis=1).reshape(trans_own.shape)

    def remote(src, dst, send, recv, **peer):
        return pltpu.make_async_remote_copy(
            src_ref=src, dst_ref=dst, send_sem=send, recv_sem=recv, device_id=peer, device_id_type=MESH
        )

    def first_copy(c, i, side):
        return remote(
            own_t.at[side, i], par_t.at[i],
            first_send.at[c, i], first_recv.at[c, i], dir=partner,
        )

    def line_copy(c, peer, slot):
        return remote(
            own_t.at[y, peer // 2], cells[c].at[1, slot],
            line_send.at[c, peer // 2], line_recv.at[c, slot], dir=peer,
        )

    def relay_copy(c, peer, slot):
        return remote(
            par_t.at[peer // 2], cells[c].at[1, slot],
            relay_send.at[c, peer // 2], line_recv.at[c, slot], dir=peer,
        )

    def tr_copy(peer, slot):
        return remote(
            trans_own.at[share], trans_all.at[slot, share], tr_send.at[peer], tr_recv.at[slot], dir=peer
        )

    def ts_copy(peer, slot):
        return remote(
            trans_all.at[:, slot], trans_all.at[:, slot], ts_send.at[peer], ts_recv.at[slot], slab=peer
        )

    def slab_copy(c, side, d):
        target = slab + 1 if side == 0 else slab - 1
        return remote(
            cells[c].at[1, d], cells[c].at[2 * side, d],
            slab_send.at[c, side, d], slab_recv.at[c, side, d], slab=target,
        )

    def nb_copy(side):
        lanes = pl.ds(pl.multiple_of(side * hr, 128), hr)
        return remote(
            cur.at[:, :, :, lanes], near_par.at[:, :, :, lanes], nb_send, nb_recv, dir=partner
        )

    def ng_copy(c, d, holder):
        return remote(
            cells[c].at[1, d], near_turned.at[lax.rem(holder, 2), holder // 2],
            ng_send.at[c, d], ng_recv.at[c, holder], dir=across(d),
        )

    def apart(target):
        return pl.ds((1 - target // 2 // zh) * zh, zh)

    def na_copy(c, side, target, peer):
        window = apart(target)
        return remote(
            own_t.at[side, window], near_turned.at[side, window], na_send.at[c], na_recv.at[c], dir=peer
        )

    def nr_copy(c, side, target, peer):
        return remote(
            par_t.at[apart(target)], near_turned.at[side, apart(target)],
            nr_send.at[c], nr_recv.at[c], dir=peer,
        )

    def ret_copy(c, peer, sender):
        return remote(
            far_out[c].at[peer], far_all.at[lax.rem(sender, 2), sender // 2],
            ret_send.at[c, peer], ret_recv.at[c, sender], dir=peer,
        )

    def same_half(d):
        return d // 2 // zh == z // zh

    def passes_on(d):
        return jnp.logical_and(same_half(across(d)), across(d) != me)

    def forward(c, d):
        @pl.when(has_next)
        def _():
            slab_copy(c, 0, d).start()

        @pl.when(has_prev)
        def _():
            slab_copy(c, 1, d).start()

    def spare(c, inside):
        @pl.when(same_half(across(me)) == inside)
        def _():
            na_copy(c, y, across(me), across(me)).start()

        @pl.when(same_half(across(partner)) == inside)
        def _():
            nr_copy(c, y, across(partner), across(partner)).start()

    def stage(s):
        @pl.when(has_upper)
        def _():
            greet(hand.at[s, 0], me + 2)

        @pl.when(has_lower)
        def _():
            greet(hand.at[s, 1], me - 2)

    def staged(s):
        @pl.when(has_lower)
        def _():
            pl.semaphore_wait(hand.at[s, 0], 1)

        @pl.when(has_upper)
        def _():
            pl.semaphore_wait(hand.at[s, 1], 1)

    def along(o):
        @pl.when(z + o < zs)
        def _():
            tr_copy(me + 2 * o, me).start()
            for c in range(len(chunks)):
                line_copy(c, me + 2 * o, me).start()

        @pl.when(z - o >= 0)
        def _():
            tr_copy(me - 2 * o, me).start()
            for c in range(len(chunks)):
                line_copy(c, me - 2 * o, me).start()

    def askew(o):
        @pl.when(z + o < zs)
        def _():
            tr_copy(partner + 2 * o, me).start()

        @pl.when(z - o >= 0)
        def _():
            tr_copy(partner - 2 * o, me).start()

    pl.semaphore_wait(barrier, slabs + (z + zs - 1) // zs + (2 * zs - 2 - z) // zs)
    stage(0)
    for c, (nz, rc, off) in enumerate(chunks):
        for o in range(nz):
            first_copy(c, lax.rem(toward(o + 1), nz), 1 - y).start()
    tr_copy(partner, me).start()
    along(1)
    nb_copy(y).start()
    for c in range(len(chunks)):
        cells[c][1, me] = own_t[y, z]
        forward(c, me)
    for o in range(2, zs):
        staged(o - 2)
        stage(o - 1)
        askew(o - 1)
        along(o)
    staged(zs - 2)
    askew(zs - 1)

    for copy in later_copies:
        copy.wait()
    agg_hi[...], agg_lo[...] = split(complex_weights(aggregate[0].T, aggregate[1].T))
    dis_hi[...], dis_lo[...] = split(complex_weights(disaggregate[0].T, disaggregate[1].T))

    for c, (nz, rc, off) in enumerate(chunks):
        for o in range(nz):
            i = lax.rem(toward(o + 1), nz)
            first_copy(c, i, 1 - y).wait_recv()
            for g in range(zs // nz):
                @pl.when(i + g * nz != z)
                def _():
                    relay_copy(c, 2 * (i + g * nz) + y, partner).start()

        if nz == zs:
            spare(c, True)
        cells[c][1, partner] = par_t[z]
        forward(c, partner)

    trans_all[me, share] = trans_own[share]

    @pl.when(jnp.logical_not(has_prev))
    def _():
        for c in range(len(chunks)):
            cells[c][0] = jnp.zeros_like(cells[c][0])

    @pl.when(jnp.logical_not(has_next))
    def _():
        for c in range(len(chunks)):
            cells[c][2] = jnp.zeros_like(cells[c][2])

    lines = 2 * (zs - 1)
    steps = lines * len(chunks)

    def take(c, q):
        peer = 2 * toward(1 + lax.rem(q, zs - 1)) + lax.rem(y + q // (zs - 1), 2)
        line_copy(c, peer, peer).wait_recv()
        forward(c, peer)
        split_near(c * lines + q)

    def near_starts():
        for c, (nz, rc, off) in enumerate(chunks):
            if nz == zs:
                spare(c, False)

            @pl.loop(0, dirs)
            def _(d):
                @pl.when(passes_on(d))
                def _():
                    ng_copy(c, d, me).start()
    load = -(-box_dev * nn // steps)

    def split_near(t):
        @pl.loop(t * load, jnp.minimum((t + 1) * load, box_dev * nn))
        def _(q):
            b, j = q // nn, lax.rem(q, nn)
            pair = jnp.concatenate([near_blocks[0, b, j], near_blocks[1, b, j]], axis=1)
            near_hi[b, j], near_lo[b, j] = split(pair)

    def joined(ref, part, b):
        return jnp.concatenate([ref[i, part, b] for i in range(zs)], axis=0).T

    def whole(ref, part, b):
        return jnp.concatenate([ref[d // zs, d % zs, part, b] for d in range(dirs)], axis=0).T

    def near_weights(group, b, real, imag):
        w_hi[group * box_dev + b], w_lo[group * box_dev + b] = split(complex_weights(real, imag))

    def radiate(c, g):
        rc = chunks[c][1]
        count = dirs * box_dev * rc
        pair = jnp.concatenate(
            [cells[c][g, :, part].reshape(count, p_size) for part in range(2)], axis=1
        )
        w = dot3(split(pair), (agg_hi[...], agg_lo[...]))
        re = w[:, :k_size].reshape(slab_boxes, rc // 8, 8, k_size)
        im = w[:, k_size:].reshape(slab_boxes, rc // 8, 8, k_size)
        boxes = pl.ds(g * slab_boxes, slab_boxes)
        x[c][0, boxes] = re
        x[c][1, boxes] = im
        x[c][2, boxes] = re + im

    def far_device(c, owner):
        rc = chunks[c][1]
        step = min(rc // 8, 4)
        for bb in range(box_dev):
            b = owner * box_dev + bb
            for r in range(0, rc // 8, step):
                block = pl.ds(r, step)

                def entry(i, sums):
                    s1, s2, s3 = sums
                    src = inter_source[b, i]
                    shift = inter_shift[b, i]
                    s1 = s1 + tables[0, shift] * x[c][2, src, block]
                    s2 = s2 + tables[1, shift] * x[c][1, src, block]
                    s3 = s3 + tables[2, shift] * x[c][0, src, block]
                    return s1, s2, s3

                zero = jnp.zeros((step, 8, k_size), jnp.float32)
                s1, s2, s3 = lax.fori_loop(0, ni, entry, (zero, zero, zero), unroll=4)
                here = slice(bb * rc + 8 * r, bb * rc + 8 * (r + step))
                inc[c][here, :k_size] = (s1 - s2).reshape(8 * step, k_size)
                inc[c][here, k_size:] = (s1 + s3).reshape(8 * step, k_size)
        w = dot3(split(inc[c][...]), (dis_hi[...], dis_lo[...]))
        far_out[c][owner, 0] = w[:, :p_size].reshape(box_dev, rc, p_size)
        far_out[c][owner, 1] = w[:, p_size:].reshape(box_dev, rc, p_size)

    for c, (nz, rc, off) in enumerate(chunks):
        if c == 0:
            @pl.loop(0, zs - 1)
            def _(q):
                take(0, q)

            @pl.loop(1, dirs)
            def _(o):
                peer = lax.rem(me + dirs - o, dirs)
                tr_copy(peer, peer).wait_recv()

            if shares > 1:
                @pl.loop(1, slabs)
                def _(o):
                    ts_copy(lax.rem(slab + o, slabs), slab).start()

            @pl.loop(zs - 1, lines)
            def _(q):
                take(0, q)

        if c == len(chunks) - 1:
            near_starts()

        if c == 0:
            if shares > 1:
                @pl.loop(1, slabs)
                def _(o):
                    peer = lax.rem(slab + slabs - o, slabs)
                    ts_copy(peer, peer).wait_recv()

            turned = trans_all[...].reshape(k_size, 2 * nt).T
            rows[0] = turned[:nt]
            rows[1] = turned[:nt] + turned[nt:]
            rows[2] = turned[nt:] - turned[:nt]

            @pl.loop(0, nt)
            def _(t):
                for f in range(3):
                    tables[f, t] = jnp.broadcast_to(rows[f, pl.ds(t, 1), :], (8, k_size))

        radiate(c, 1)

        if c == 0:
            for side in range(2):
                @pl.when(y == side)
                def _():
                    for part in range(2):
                        for b in range(box_dev):
                            near_par[part, b, :, side * hr:(side + 1) * hr] = joined(par_t, part, b)

            nb_copy(1 - y).wait_recv()
            for b in range(box_dev):
                near_weights(1, b, cur[0, b], cur[1, b])
                near_weights(2 - 2 * y, b, near_par[0, b], near_par[1, b])

        @pl.when(has_prev)
        def _():
            @pl.loop(0, dirs)
            def _(d):
                slab_copy(c, 0, d).wait_recv()

        radiate(c, 0)

        @pl.when(has_next)
        def _():
            @pl.loop(0, dirs)
            def _(d):
                slab_copy(c, 1, d).wait_recv()

        radiate(c, 2)
        group = 2 * nz
        base = me // group * group

        @pl.loop(0, group)
        def _(o):
            owner = base + 2 * lax.rem(toward(1 + o // 2), nz) + lax.rem(y + 1 + o, 2)
            far_device(c, owner)

            @pl.when(owner != me)
            def _():
                ret_copy(c, owner, me).start()

            if c + 1 < len(chunks):
                each = -(-lines // group)

                @pl.loop(o * each, jnp.minimum((o + 1) * each, lines))
                def _(q):
                    take(c + 1, q)

        far_all[y, z] = far_out[c][me]

    for c, (nz, rc, off) in enumerate(chunks):
        near_turned[y, z] = cells[c][1, across(me)]

        @pl.loop(0, 2 * zh)
        def _(o):
            holder = z // zh * zh * 2 + o

            @pl.when(holder != me)
            def _():
                ng_copy(c, across(me), holder).wait_recv()

        if nz == zs:
            na_copy(c, 1 - y, me, across(me)).wait_recv()
            nr_copy(c, y, me, across(me)).wait_recv()

    for b in range(box_dev):
        near_weights(2 * y, b, whole(near_turned, 0, b), whole(near_turned, 1, b))

    @pl.loop(0, box_dev)
    def _(b):
        total = jnp.zeros((p_size, 2 * illum), jnp.float32)
        for j in range(nn):
            src = near_index[b, j]
            total = total + dot3((near_hi[b, j], near_lo[b, j]), (w_hi[src], w_lo[src]))
        out[0, b] = total[:, :illum]
        out[1, b] = total[:, illum:]

    for c, (nz, rc, off) in enumerate(chunks):
        group = 2 * nz
        base = me // group * group

        @pl.loop(1, group)
        def _(o):
            peer = base + lax.rem(me + group - o, group)
            ret_copy(c, peer, peer).wait_recv()

    for part in range(2):
        for b in range(box_dev):
            out[part, b] += whole(far_all, part, b)

    for c, (nz, rc, off) in enumerate(chunks):
        group = 2 * nz
        base = me // group * group

        @pl.loop(1, group)
        def _(o):
            ret_copy(c, base + lax.rem(me + o, group), me).wait_send()

        @pl.loop(0, nz)
        def _(i):
            first_copy(c, i, 1 - y).wait_send()

        @pl.loop(1, zs)
        def _(o):
            peer = 2 * lax.rem(z + o, zs) + y
            line_copy(c, peer, me).wait_send()
            relay_copy(c, peer, partner).wait_send()

        @pl.loop(0, dirs)
        def _(d):
            @pl.when(passes_on(d))
            def _():
                ng_copy(c, d, me).wait_send()

        if nz == zs:
            na_copy(c, y, across(me), across(me)).wait_send()
            nr_copy(c, y, across(partner), across(partner)).wait_send()

        @pl.when(has_next)
        def _():
            @pl.loop(0, dirs)
            def _(d):
                slab_copy(c, 0, d).wait_send()

        @pl.when(has_prev)
        def _():
            @pl.loop(0, dirs)
            def _(d):
                slab_copy(c, 1, d).wait_send()

    @pl.loop(1, dirs)
    def _(o):
        tr_copy(lax.rem(me + o, dirs), me).wait_send()

    if shares > 1:
        @pl.loop(1, slabs)
        def _(o):
            ts_copy(lax.rem(slab + o, slabs), slab).wait_send()

    nb_copy(y).wait_send()


def body(slabs, dirs, *args):
    cur, near_blocks, near_index, aggregate, trans, inter_source, inter_shift, disaggregate = args
    box_dev, p_size, illum = cur.shape[1:]
    nn = near_blocks.shape[2]
    k_size = aggregate.shape[1]
    nt, k_loc = trans.shape[1:]
    slab_boxes = inter_source.shape[0]
    zs = dirs // 2
    chunks = plan(illum, zs)
    n = len(chunks)
    shares = slabs if k_loc % (8 * slabs) == 0 else 1
    f32, bf16 = jnp.float32, jnp.bfloat16
    vmem = pl.BlockSpec(memory_space=pltpu.VMEM)
    sem = pltpu.SemaphoreType.DMA
    turned = pltpu.VMEM((2, zs, 2, box_dev, illum // dirs, p_size), f32)
    operands = (
        cur, near_blocks, near_index, aggregate, jnp.swapaxes(trans, 1, 2), inter_source, inter_shift, disaggregate
    )
    return pl.pallas_call(
        functools.partial(kernel, slabs, dirs, chunks),
        out_shape=jax.ShapeDtypeStruct(cur.shape, f32),
        in_specs=[pl.BlockSpec(memory_space=pltpu.HBM)] * 8,
        out_specs=vmem,
        scratch_shapes=[
            pltpu.VMEM(cur.shape, f32),
            pltpu.SMEM(near_index.shape, jnp.int32),
            pltpu.VMEM(aggregate.shape, f32),
            pltpu.VMEM((2, k_loc, nt), f32),
            pltpu.SMEM(inter_source.shape, jnp.int32),
            pltpu.SMEM(inter_shift.shape, jnp.int32),
            pltpu.VMEM(disaggregate.shape, f32),
            sem((8,)),
            pltpu.VMEM(near_blocks.shape, f32),
            pltpu.VMEM((box_dev, nn, p_size, 2 * p_size), bf16),
            pltpu.VMEM((box_dev, nn, p_size, 2 * p_size), bf16),
            pltpu.VMEM(cur.shape, f32),
            turned,
            pltpu.VMEM((3 * box_dev, 2 * p_size, 2 * illum), bf16),
            pltpu.VMEM((3 * box_dev, 2 * p_size, 2 * illum), bf16),
            turned,
            pltpu.VMEM((zs, 2, box_dev, illum // dirs, p_size), f32),
            turned,
            pltpu.VMEM((shares, k_loc // shares, 2 * nt), f32),
            pltpu.VMEM((dirs, shares, k_loc // shares, 2 * nt), f32),
            pltpu.VMEM((3, nt, k_size), f32),
            pltpu.VMEM((3, nt, 8, k_size), f32),
            pltpu.VMEM((2 * p_size, 2 * k_size), bf16),
            pltpu.VMEM((2 * p_size, 2 * k_size), bf16),
            pltpu.VMEM((2 * k_size, 2 * p_size), bf16),
            pltpu.VMEM((2 * k_size, 2 * p_size), bf16),
            [pltpu.VMEM((3, dirs, 2, box_dev, rc, p_size), f32) for _, rc, _ in chunks],
            [pltpu.VMEM((3, 3 * slab_boxes, rc // 8, 8, k_size), f32) for _, rc, _ in chunks],
            [pltpu.VMEM((box_dev * rc, 2 * k_size), f32) for _, rc, _ in chunks],
            [pltpu.VMEM((dirs, 2, box_dev, rc, p_size), f32) for _, rc, _ in chunks],
            pltpu.SemaphoreType.REGULAR((zs, 2)),
            sem((n, zs)), sem((n, zs)),
            sem((n, zs)), sem((n, zs)), sem((n, dirs)),
            sem((n, 2, dirs)), sem((n, 2, dirs)),
            sem((dirs,)), sem((dirs,)),
            sem((slabs,)), sem((slabs,)),
            sem(()), sem(()),
            sem((n, dirs)), sem((n, dirs)),
            sem((n,)), sem((n,)),
            sem((n,)), sem((n,)),
            sem((n, dirs)), sem((n, dirs)),
        ],
        compiler_params=pltpu.CompilerParams(
            collective_id=0, has_side_effects=True, vmem_limit_bytes=48 * 2**20
        ),
    )(*[pltpu.with_memory_space_constraint(v, pltpu.HBM) for v in operands])


def solution(mesh):
    in_specs = (
        P(None, ("slab", "dir"), None, None),
        P(None, ("slab", "dir"), None, None, None),
        P(("slab", "dir"), None),
        P(),
        P(None, None, "dir"),
        P("slab", None),
        P("slab", None),
        P(),
    )
    out_specs = P(None, ("slab", "dir"), None, None)
    run = functools.partial(body, mesh.shape["slab"], mesh.shape["dir"])
    return jax.shard_map(run, mesh=mesh, in_specs=in_specs, out_specs=out_specs, check_vma=False)
```

```python
import functools

import jax
import jax.numpy as jnp
from jax import lax
from jax.experimental import pallas as pl
from jax.experimental.pallas import tpu as pltpu
from jax.sharding import PartitionSpec as P

MESH = pl.DeviceIdType.MESH


def split(x):
    hi = x.astype(jnp.bfloat16)
    lo = (x - hi.astype(jnp.float32)).astype(jnp.bfloat16)
    return hi, lo


def dot3(left, right):
    def single(u, v):
        return jnp.dot(u, v, preferred_element_type=jnp.float32)

    return single(left[0], right[0]) + (single(left[0], right[1]) + single(left[1], right[0]))


def complex_weights(real, imag):
    return jnp.concatenate(
        [jnp.concatenate([real, imag], axis=1), jnp.concatenate([-imag, real], axis=1)], axis=0
    )


def plan(illum, zs):
    half = illum // 2
    return ((zs, half // zs, 0),)


def kernel(
    slabs, dirs, chunks,
    cur_hbm, near_hbm, near_index_hbm, aggregate_hbm, trans_hbm, source_hbm, shift_hbm, disaggregate_hbm,
    out,
    cur, near_index, aggregate, trans, inter_source, inter_shift, disaggregate, input_sem,
    near_blocks, near_hi, near_lo, near_par, near_turned, w_hi, w_lo,
    own_t, par_t, far_all, trans_own, trans_all, rows, tables, agg_hi, agg_lo, dis_hi, dis_lo,
    cells, x, inc, far_out,
    hand, first_send, first_recv, line_send, relay_send, line_recv, slab_send, slab_recv,
    tr_send, tr_recv, ts_send, ts_recv, nb_send, nb_recv, ng_send, ng_recv,
    na_send, na_recv, nr_send, nr_recv, ret_send, ret_recv,
):
    slab = lax.axis_index("slab")
    me = lax.axis_index("dir")
    box_dev, p_size, illum = cur.shape[1:]
    nn = near_hbm.shape[2]
    k_size = aggregate.shape[1]
    nt = trans.shape[2]
    slab_boxes, ni = inter_source.shape
    has_prev = slab > 0
    has_next = slab < slabs - 1
    shares = trans_all.shape[1]
    share = slab if shares > 1 else 0
    zs = dirs // 2
    zh = zs // 2
    hr = illum // 2
    rc0 = illum // dirs
    z = me // 2
    y = lax.rem(me, 2)
    partner = 2 * z + 1 - y
    has_lower = z > 0
    has_upper = z < zs - 1
    inward = 1 - 2 * (z // zh)

    def toward(o):
        return lax.rem(z + inward * o + zs, zs)

    def across(d):
        return lax.rem(d + 2 * lax.rem(d, 2) - 1 + dirs, dirs)

    barrier = pltpu.get_barrier_semaphore()

    def greet(sem, peer):
        pl.semaphore_signal(sem, inc=1, device_id={"dir": peer}, device_id_type=MESH)

    greet(barrier, partner)

    @pl.when(has_lower)
    def _():
        greet(barrier, me - 2)

    @pl.when(has_upper)
    def _():
        greet(barrier, me + 2)

    @pl.loop(1, slabs)
    def _(o):
        pl.semaphore_signal(barrier, inc=1, device_id={"slab": lax.rem(slab + o, slabs)}, device_id_type=MESH)

    cur_copy, trans_copy, *later_copies = [
        pltpu.make_async_copy(source, target, input_sem.at[i])
        for i, (source, target) in enumerate([
            (cur_hbm, cur), (trans_hbm, trans), (aggregate_hbm, aggregate),
            (disaggregate_hbm, disaggregate), (source_hbm, inter_source),
            (shift_hbm, inter_shift), (near_index_hbm, near_index), (near_hbm, near_blocks),
        ])
    ]
    cur_copy.start()
    trans_copy.start()
    for copy in later_copies:
        copy.start()
    cur_copy.wait()

    for part in range(2):
        for b in range(box_dev):
            turned = cur[part, b].T
            for d in range(dirs):
                own_t[d // zs, d % zs, part, b] = turned[d * rc0:(d + 1) * rc0]
    trans_copy.wait()
    trans_own[...] = jnp.concatenate([trans[0], trans[1]], axis=1).reshape(trans_own.shape)

    def remote(src, dst, send, recv, **peer):
        return pltpu.make_async_remote_copy(
            src_ref=src, dst_ref=dst, send_sem=send, recv_sem=recv, device_id=peer, device_id_type=MESH
        )

    def first_copy(c, i, side):
        return remote(
            own_t.at[side, i], par_t.at[i],
            first_send.at[c, i], first_recv.at[c, i], dir=partner,
        )

    def line_copy(c, peer, slot):
        return remote(
            own_t.at[y, peer // 2], cells[c].at[1, slot],
            line_send.at[c, peer // 2], line_recv.at[c, slot], dir=peer,
        )

    def relay_copy(c, peer, slot):
        return remote(
            par_t.at[peer // 2], cells[c].at[1, slot],
            relay_send.at[c, peer // 2], line_recv.at[c, slot], dir=peer,
        )

    def tr_copy(peer, slot):
        return remote(
            trans_own.at[share], trans_all.at[slot, share], tr_send.at[peer], tr_recv.at[slot], dir=peer
        )

    def ts_copy(peer, slot):
        return remote(
            trans_all.at[:, slot], trans_all.at[:, slot], ts_send.at[peer], ts_recv.at[slot], slab=peer
        )

    def slab_copy(c, side, d):
        target = slab + 1 if side == 0 else slab - 1
        return remote(
            cells[c].at[1, d], cells[c].at[2 * side, d],
            slab_send.at[c, side, d], slab_recv.at[c, side, d], slab=target,
        )

    def nb_copy(side):
        lanes = pl.ds(pl.multiple_of(side * hr, 128), hr)
        return remote(
            cur.at[:, :, :, lanes], near_par.at[:, :, :, lanes], nb_send, nb_recv, dir=partner
        )

    def ng_copy(c, d, holder):
        return remote(
            cells[c].at[1, d], near_turned.at[lax.rem(holder, 2), holder // 2],
            ng_send.at[c, d], ng_recv.at[c, holder], dir=across(d),
        )

    def apart(target):
        return pl.ds((1 - target // 2 // zh) * zh, zh)

    def na_copy(c, side, target, peer):
        window = apart(target)
        return remote(
            own_t.at[side, window], near_turned.at[side, window], na_send.at[c], na_recv.at[c], dir=peer
        )

    def nr_copy(c, side, target, peer):
        return remote(
            par_t.at[apart(target)], near_turned.at[side, apart(target)],
            nr_send.at[c], nr_recv.at[c], dir=peer,
        )

    def ret_copy(c, peer, sender):
        return remote(
            far_out[c].at[peer], far_all.at[lax.rem(sender, 2), sender // 2],
            ret_send.at[c, peer], ret_recv.at[c, sender], dir=peer,
        )

    def same_half(d):
        return d // 2 // zh == z // zh

    def passes_on(d):
        return jnp.logical_and(same_half(across(d)), across(d) != me)

    def forward(c, d):
        @pl.when(has_next)
        def _():
            slab_copy(c, 0, d).start()

        @pl.when(has_prev)
        def _():
            slab_copy(c, 1, d).start()

    def spare(c, inside):
        @pl.when(same_half(across(me)) == inside)
        def _():
            na_copy(c, y, across(me), across(me)).start()

        @pl.when(same_half(across(partner)) == inside)
        def _():
            nr_copy(c, y, across(partner), across(partner)).start()

    def stage(s):
        @pl.when(has_upper)
        def _():
            greet(hand.at[s, 0], me + 2)

        @pl.when(has_lower)
        def _():
            greet(hand.at[s, 1], me - 2)

    def staged(s):
        @pl.when(has_lower)
        def _():
            pl.semaphore_wait(hand.at[s, 0], 1)

        @pl.when(has_upper)
        def _():
            pl.semaphore_wait(hand.at[s, 1], 1)

    def along(o):
        @pl.when(z + o < zs)
        def _():
            tr_copy(me + 2 * o, me).start()
            for c in range(len(chunks)):
                line_copy(c, me + 2 * o, me).start()

        @pl.when(z - o >= 0)
        def _():
            tr_copy(me - 2 * o, me).start()
            for c in range(len(chunks)):
                line_copy(c, me - 2 * o, me).start()

    def askew(o):
        @pl.when(z + o < zs)
        def _():
            tr_copy(partner + 2 * o, me).start()

        @pl.when(z - o >= 0)
        def _():
            tr_copy(partner - 2 * o, me).start()

    pl.semaphore_wait(barrier, slabs + (z + zs - 1) // zs + (2 * zs - 2 - z) // zs)
    stage(0)
    for c, (nz, rc, off) in enumerate(chunks):
        for o in range(nz):
            first_copy(c, lax.rem(toward(o + 1), nz), 1 - y).start()
    tr_copy(partner, me).start()
    along(1)
    nb_copy(y).start()
    for c in range(len(chunks)):
        cells[c][1, me] = own_t[y, z]
        forward(c, me)
    for o in range(2, zs):
        staged(o - 2)
        stage(o - 1)
        askew(o - 1)
        along(o)
    staged(zs - 2)
    askew(zs - 1)

    for copy in later_copies:
        copy.wait()
    agg_hi[...], agg_lo[...] = split(complex_weights(aggregate[0].T, aggregate[1].T))
    dis_hi[...], dis_lo[...] = split(complex_weights(disaggregate[0].T, disaggregate[1].T))

    lines = 2 * (zs - 1)
    steps = zs - 1

    def take(c, q):
        peer = 2 * toward(1 + lax.rem(q, zs - 1)) + lax.rem(y + q // (zs - 1), 2)
        line_copy(c, peer, peer).wait_recv()
        forward(c, peer)

    for c, (nz, rc, off) in enumerate(chunks):
        for o in range(nz):
            i = lax.rem(toward(o + 1), nz)
            first_copy(c, i, 1 - y).wait_recv()
            for g in range(zs // nz):
                @pl.when(i + g * nz != z)
                def _():
                    relay_copy(c, 2 * (i + g * nz) + y, partner).start()

            if o < zs - 1:
                take(0, o)

        if nz == zs:
            spare(c, True)
        cells[c][1, partner] = par_t[z]
        forward(c, partner)

    trans_all[me, share] = trans_own[share]

    @pl.when(jnp.logical_not(has_prev))
    def _():
        for c in range(len(chunks)):
            cells[c][0] = jnp.zeros_like(cells[c][0])

    @pl.when(jnp.logical_not(has_next))
    def _():
        for c in range(len(chunks)):
            cells[c][2] = jnp.zeros_like(cells[c][2])

    def near_starts():
        for c, (nz, rc, off) in enumerate(chunks):
            if nz == zs:
                spare(c, False)

            @pl.loop(0, dirs)
            def _(d):
                @pl.when(passes_on(d))
                def _():
                    ng_copy(c, d, me).start()
    load = -(-box_dev * nn // steps)

    def split_near(t):
        @pl.loop(t * load, jnp.minimum((t + 1) * load, box_dev * nn))
        def _(q):
            b, j = q // nn, lax.rem(q, nn)
            pair = jnp.concatenate([near_blocks[0, b, j], near_blocks[1, b, j]], axis=1)
            near_hi[b, j], near_lo[b, j] = split(pair)

    def joined(ref, part, b):
        return jnp.concatenate([ref[i, part, b] for i in range(zs)], axis=0).T

    def whole(ref, part, b):
        return jnp.concatenate([ref[d // zs, d % zs, part, b] for d in range(dirs)], axis=0).T

    def near_weights(group, b, real, imag):
        w_hi[group * box_dev + b], w_lo[group * box_dev + b] = split(complex_weights(real, imag))

    def radiate(c, g):
        rc = chunks[c][1]
        count = dirs * box_dev * rc
        pair = jnp.concatenate(
            [cells[c][g, :, part].reshape(count, p_size) for part in range(2)], axis=1
        )
        w = dot3(split(pair), (agg_hi[...], agg_lo[...]))
        re = w[:, :k_size].reshape(slab_boxes, rc // 8, 8, k_size)
        im = w[:, k_size:].reshape(slab_boxes, rc // 8, 8, k_size)
        boxes = pl.ds(g * slab_boxes, slab_boxes)
        x[c][0, boxes] = re
        x[c][1, boxes] = im
        x[c][2, boxes] = re + im

    def far_device(c, owner):
        rc = chunks[c][1]
        step = min(rc // 8, 4)
        for bb in range(box_dev):
            b = owner * box_dev + bb
            for r in range(0, rc // 8, step):
                block = pl.ds(r, step)

                def entry(i, sums):
                    s1, s2, s3 = sums
                    src = inter_source[b, i]
                    shift = inter_shift[b, i]
                    s1 = s1 + tables[0, shift] * x[c][2, src, block]
                    s2 = s2 + tables[1, shift] * x[c][1, src, block]
                    s3 = s3 + tables[2, shift] * x[c][0, src, block]
                    return s1, s2, s3

                zero = jnp.zeros((step, 8, k_size), jnp.float32)
                s1, s2, s3 = lax.fori_loop(0, ni, entry, (zero, zero, zero), unroll=4)
                here = slice(bb * rc + 8 * r, bb * rc + 8 * (r + step))
                inc[c][here, :k_size] = (s1 - s2).reshape(8 * step, k_size)
                inc[c][here, k_size:] = (s1 + s3).reshape(8 * step, k_size)
        w = dot3(split(inc[c][...]), (dis_hi[...], dis_lo[...]))
        far_out[c][owner, 0] = w[:, :p_size].reshape(box_dev, rc, p_size)
        far_out[c][owner, 1] = w[:, p_size:].reshape(box_dev, rc, p_size)

    for c, (nz, rc, off) in enumerate(chunks):
        if c == 0:
            @pl.loop(1, dirs)
            def _(o):
                peer = lax.rem(me + dirs - o, dirs)
                tr_copy(peer, peer).wait_recv()

            if shares > 1:
                @pl.loop(1, slabs)
                def _(o):
                    ts_copy(lax.rem(slab + o, slabs), slab).start()

            @pl.loop(zs - 1, lines)
            def _(q):
                take(0, q)
                split_near(q - zs + 1)

        if c == len(chunks) - 1:
            near_starts()

        if c == 0:
            if shares > 1:
                @pl.loop(1, slabs)
                def _(o):
                    peer = lax.rem(slab + slabs - o, slabs)
                    ts_copy(peer, peer).wait_recv()

            turned = trans_all[...].reshape(k_size, 2 * nt).T
            rows[0] = turned[:nt]
            rows[1] = turned[:nt] + turned[nt:]
            rows[2] = turned[nt:] - turned[:nt]

            @pl.loop(0, nt)
            def _(t):
                for f in range(3):
                    tables[f, t] = jnp.broadcast_to(rows[f, pl.ds(t, 1), :], (8, k_size))

        radiate(c, 1)

        if c == 0:
            for side in range(2):
                @pl.when(y == side)
                def _():
                    for part in range(2):
                        for b in range(box_dev):
                            near_par[part, b, :, side * hr:(side + 1) * hr] = joined(par_t, part, b)

            nb_copy(1 - y).wait_recv()
            for b in range(box_dev):
                near_weights(1, b, cur[0, b], cur[1, b])
                near_weights(2 - 2 * y, b, near_par[0, b], near_par[1, b])

        @pl.when(has_prev)
        def _():
            @pl.loop(0, dirs)
            def _(d):
                slab_copy(c, 0, d).wait_recv()

        radiate(c, 0)

        @pl.when(has_next)
        def _():
            @pl.loop(0, dirs)
            def _(d):
                slab_copy(c, 1, d).wait_recv()

        radiate(c, 2)
        group = 2 * nz
        base = me // group * group

        @pl.loop(0, group)
        def _(o):
            owner = base + 2 * lax.rem(toward(1 + o // 2), nz) + lax.rem(y + 1 + o, 2)
            far_device(c, owner)

            @pl.when(owner != me)
            def _():
                ret_copy(c, owner, me).start()

            if c + 1 < len(chunks):
                each = -(-lines // group)

                @pl.loop(o * each, jnp.minimum((o + 1) * each, lines))
                def _(q):
                    take(c + 1, q)

        far_all[y, z] = far_out[c][me]

    for c, (nz, rc, off) in enumerate(chunks):
        near_turned[y, z] = cells[c][1, across(me)]

        @pl.loop(0, 2 * zh)
        def _(o):
            holder = z // zh * zh * 2 + o

            @pl.when(holder != me)
            def _():
                ng_copy(c, across(me), holder).wait_recv()

        if nz == zs:
            na_copy(c, 1 - y, me, across(me)).wait_recv()
            nr_copy(c, y, me, across(me)).wait_recv()

    for b in range(box_dev):
        near_weights(2 * y, b, whole(near_turned, 0, b), whole(near_turned, 1, b))

    @pl.loop(0, box_dev)
    def _(b):
        total = jnp.zeros((p_size, 2 * illum), jnp.float32)
        for j in range(nn):
            src = near_index[b, j]
            total = total + dot3((near_hi[b, j], near_lo[b, j]), (w_hi[src], w_lo[src]))
        out[0, b] = total[:, :illum]
        out[1, b] = total[:, illum:]

    for c, (nz, rc, off) in enumerate(chunks):
        group = 2 * nz
        base = me // group * group

        @pl.loop(1, group)
        def _(o):
            peer = base + lax.rem(me + group - o, group)
            ret_copy(c, peer, peer).wait_recv()

    for part in range(2):
        for b in range(box_dev):
            out[part, b] += whole(far_all, part, b)

    for c, (nz, rc, off) in enumerate(chunks):
        group = 2 * nz
        base = me // group * group

        @pl.loop(1, group)
        def _(o):
            ret_copy(c, base + lax.rem(me + o, group), me).wait_send()

        @pl.loop(0, nz)
        def _(i):
            first_copy(c, i, 1 - y).wait_send()

        @pl.loop(1, zs)
        def _(o):
            peer = 2 * lax.rem(z + o, zs) + y
            line_copy(c, peer, me).wait_send()
            relay_copy(c, peer, partner).wait_send()

        @pl.loop(0, dirs)
        def _(d):
            @pl.when(passes_on(d))
            def _():
                ng_copy(c, d, me).wait_send()

        if nz == zs:
            na_copy(c, y, across(me), across(me)).wait_send()
            nr_copy(c, y, across(partner), across(partner)).wait_send()

        @pl.when(has_next)
        def _():
            @pl.loop(0, dirs)
            def _(d):
                slab_copy(c, 0, d).wait_send()

        @pl.when(has_prev)
        def _():
            @pl.loop(0, dirs)
            def _(d):
                slab_copy(c, 1, d).wait_send()

    @pl.loop(1, dirs)
    def _(o):
        tr_copy(lax.rem(me + o, dirs), me).wait_send()

    if shares > 1:
        @pl.loop(1, slabs)
        def _(o):
            ts_copy(lax.rem(slab + o, slabs), slab).wait_send()

    nb_copy(y).wait_send()


def body(slabs, dirs, *args):
    cur, near_blocks, near_index, aggregate, trans, inter_source, inter_shift, disaggregate = args
    box_dev, p_size, illum = cur.shape[1:]
    nn = near_blocks.shape[2]
    k_size = aggregate.shape[1]
    nt, k_loc = trans.shape[1:]
    slab_boxes = inter_source.shape[0]
    zs = dirs // 2
    chunks = plan(illum, zs)
    n = len(chunks)
    shares = slabs if k_loc % (8 * slabs) == 0 else 1
    f32, bf16 = jnp.float32, jnp.bfloat16
    vmem = pl.BlockSpec(memory_space=pltpu.VMEM)
    sem = pltpu.SemaphoreType.DMA
    turned = pltpu.VMEM((2, zs, 2, box_dev, illum // dirs, p_size), f32)
    operands = (
        cur, near_blocks, near_index, aggregate, jnp.swapaxes(trans, 1, 2), inter_source, inter_shift, disaggregate
    )
    return pl.pallas_call(
        functools.partial(kernel, slabs, dirs, chunks),
        out_shape=jax.ShapeDtypeStruct(cur.shape, f32),
        in_specs=[pl.BlockSpec(memory_space=pltpu.HBM)] * 8,
        out_specs=vmem,
        scratch_shapes=[
            pltpu.VMEM(cur.shape, f32),
            pltpu.SMEM(near_index.shape, jnp.int32),
            pltpu.VMEM(aggregate.shape, f32),
            pltpu.VMEM((2, k_loc, nt), f32),
            pltpu.SMEM(inter_source.shape, jnp.int32),
            pltpu.SMEM(inter_shift.shape, jnp.int32),
            pltpu.VMEM(disaggregate.shape, f32),
            sem((8,)),
            pltpu.VMEM(near_blocks.shape, f32),
            pltpu.VMEM((box_dev, nn, p_size, 2 * p_size), bf16),
            pltpu.VMEM((box_dev, nn, p_size, 2 * p_size), bf16),
            pltpu.VMEM(cur.shape, f32),
            turned,
            pltpu.VMEM((3 * box_dev, 2 * p_size, 2 * illum), bf16),
            pltpu.VMEM((3 * box_dev, 2 * p_size, 2 * illum), bf16),
            turned,
            pltpu.VMEM((zs, 2, box_dev, illum // dirs, p_size), f32),
            turned,
            pltpu.VMEM((shares, k_loc // shares, 2 * nt), f32),
            pltpu.VMEM((dirs, shares, k_loc // shares, 2 * nt), f32),
            pltpu.VMEM((3, nt, k_size), f32),
            pltpu.VMEM((3, nt, 8, k_size), f32),
            pltpu.VMEM((2 * p_size, 2 * k_size), bf16),
            pltpu.VMEM((2 * p_size, 2 * k_size), bf16),
            pltpu.VMEM((2 * k_size, 2 * p_size), bf16),
            pltpu.VMEM((2 * k_size, 2 * p_size), bf16),
            [pltpu.VMEM((3, dirs, 2, box_dev, rc, p_size), f32) for _, rc, _ in chunks],
            [pltpu.VMEM((3, 3 * slab_boxes, rc // 8, 8, k_size), f32) for _, rc, _ in chunks],
            [pltpu.VMEM((box_dev * rc, 2 * k_size), f32) for _, rc, _ in chunks],
            [pltpu.VMEM((dirs, 2, box_dev, rc, p_size), f32) for _, rc, _ in chunks],
            pltpu.SemaphoreType.REGULAR((zs, 2)),
            sem((n, zs)), sem((n, zs)),
            sem((n, zs)), sem((n, zs)), sem((n, dirs)),
            sem((n, 2, dirs)), sem((n, 2, dirs)),
            sem((dirs,)), sem((dirs,)),
            sem((slabs,)), sem((slabs,)),
            sem(()), sem(()),
            sem((n, dirs)), sem((n, dirs)),
            sem((n,)), sem((n,)),
            sem((n,)), sem((n,)),
            sem((n, dirs)), sem((n, dirs)),
        ],
        compiler_params=pltpu.CompilerParams(
            collective_id=0, has_side_effects=True, vmem_limit_bytes=48 * 2**20
        ),
    )(*[pltpu.with_memory_space_constraint(v, pltpu.HBM) for v in operands])


def solution(mesh):
    in_specs = (
        P(None, ("slab", "dir"), None, None),
        P(None, ("slab", "dir"), None, None, None),
        P(("slab", "dir"), None),
        P(),
        P(None, None, "dir"),
        P("slab", None),
        P("slab", None),
        P(),
    )
    out_specs = P(None, ("slab", "dir"), None, None)
    run = functools.partial(body, mesh.shape["slab"], mesh.shape["dir"])
    return jax.shard_map(run, mesh=mesh, in_specs=in_specs, out_specs=out_specs, check_vma=False)
```
